32 devices in a mesh: row: 4 (over y, x), col: 8 (over z, core).
Axes of the slice: x: 2, y: 2, z: 4, core: 2. Of those that a mesh axis runs over, the one named last changes fastest.
Arguments:
- right_side: float32 [512, 128], P('row'), may hold values from -6 to 6
- factor_window: float32 [512, 512], P('row', 'col'), may hold values from -0.1875 to 0.1875
- diag_inverse: float32 [512, 128], P('row'), as said below
- phase_cov: bfloat16 [512, 16384], P('col', 'row'), may hold values from -0.25 to 0.25
Outputs:
- basis: float32 [32, 512, 128], P('row', 'col')
- solved: float32 [512, 128], P('col')
The draws below stay inside these ranges and needn't reach their ends.
Inputs may be any that keep to these rules, and one draw needn't show every extreme that they name: `diag_inverse`: each block of 128 rows is a lower triangular matrix with a diagonal between 0.5 and 2.
All inputs are finite; a program needn't handle non-finite values.
Results may differ from the reference program's by a relative error of at most 0.0043.
Values sent between devices are 32-bit elements; how exact they have to be, the bound alone decides.
A program may use at most 64 MiB of HBM per device.

```python
import jax
import jax.numpy as jnp
from jax import lax

ROWS_DEV = 128
RANK = 128
TILE_ROWS = 512
K = 512
TILES_ALL = 32
PHASE = 16384
N_ROW = 4


def draw_diag_inverse(key, part):
    first, second = jax.random.split(jax.random.fold_in(key, 7), 2)
    diagonal = jax.random.uniform(first, (K,), jnp.float32, 0.5, 2.0)
    offdiag = 0.5 * jax.random.normal(second, (K, ROWS_DEV), jnp.float32) / jnp.sqrt(jnp.float32(ROWS_DEV))
    local_row = (jnp.arange(K) % ROWS_DEV)[:, None]
    columns = jnp.arange(ROWS_DEV)[None, :]
    return jnp.where(columns < local_row, offdiag, 0.0) + jnp.where(columns == local_row, diagonal[:, None], 0.0)


def levels(stream_key, dims, cuts, smallest, high):
    def one(dim, shards_of):
        steps = jax.random.uniform(jax.random.fold_in(jax.random.fold_in(stream_key, 6), dim), (shards_of,), jnp.float32, smallest / len(cuts), high / len(cuts))
        return jnp.repeat(jnp.exp(steps), dims[dim] // shards_of).reshape((-1,) + (1,) * (len(dims) - dim - 1))

    gain = one(*cuts[0])
    for cut in cuts[1:]:
        gain = gain * one(*cut)
    return gain


def scatter_about(own_key, shape, scale, most, cuts=(), held_as=jnp.bfloat16):
    result = scale * jax.random.normal(own_key, shape, jnp.float32)
    if cuts:
        result = result * levels(own_key, shape, cuts, -0.22, 0.18)
    return jnp.clip(result, -most, most).astype(held_as)


def setup_inputs(seed: int = 0) -> dict:
    streams_of = jax.random.split(jax.random.key(seed), 5)
    right_side = scatter_about(streams_of[0], (K, RANK), 1.0, 6.0, ((0, 4),), jnp.float32)
    factor_window = scatter_about(streams_of[1], (K, K), (2 * K) ** -0.5, 0.1875, ((0, 4), (1, 8)), jnp.float32)
    diag_inverse = draw_diag_inverse(jax.random.fold_in(streams_of[4], 71), 0)
    phase_cov = scatter_about(streams_of[3], (K, PHASE), K ** -0.5, 0.25, ((0, 8), (1, 4)))
    return {"right_side": right_side, "factor_window": factor_window, "diag_inverse": diag_inverse, "phase_cov": phase_cov}


def tile_basis(lower, tile):
    return jax.scipy.linalg.solve_triangular(lower, tile.T, lower=True).T

def reference(right_side, factor_window, diag_inverse, phase_cov):
    pieces = []
    for block_index in range(N_ROW):
        start_row = block_index * ROWS_DEV
        remaining = right_side[start_row:start_row + ROWS_DEV]
        if block_index > 0:
            earlier = jnp.concatenate(pieces, axis=0)
            remaining = remaining - jnp.dot(factor_window[start_row:start_row + ROWS_DEV, :start_row].astype(jnp.float32), earlier.astype(jnp.float32), precision=lax.Precision.HIGHEST, preferred_element_type=jnp.float32)
        pieces.append(jnp.dot(diag_inverse[start_row:start_row + ROWS_DEV].astype(jnp.float32), remaining.astype(jnp.float32), precision=lax.Precision.HIGHEST, preferred_element_type=jnp.float32))
    solved = jnp.concatenate(pieces, axis=0)
    solved_low = solved.astype(jnp.bfloat16)
    weighted = jnp.dot(phase_cov.T.astype(jnp.float32), solved_low.astype(jnp.float32), preferred_element_type=jnp.float32)
    tiles = weighted.reshape(TILES_ALL, TILE_ROWS, RANK)
    gram = jnp.einsum('tsr,tsq->trq', tiles, tiles, precision=lax.Precision.HIGHEST)
    lower = jnp.linalg.cholesky(gram)
    basis = jax.vmap(tile_basis)(lower, tiles)
    return (basis, solved)
```

```python
import functools

import jax
import jax.numpy as jnp
from jax import lax
from jax.experimental import pallas as pl
from jax.experimental.pallas import tpu as pltpu
from jax.sharding import PartitionSpec as P

MESH = pl.DeviceIdType.MESH
CORES = 2
SUB = 8
F32 = jnp.float32
dot_exact = functools.partial(lax.dot_general, precision=lax.Precision.HIGHEST, preferred_element_type=F32)
NN = (((1,), (0,)), ((), ()))
NT = (((1,), (1,)), ((), ()))


def factor_inverse(gram):
    size = gram.shape[0]
    groups = size // SUB
    parts = [gram[g * SUB:(g + 1) * SUB, :] for g in range(groups)]
    lane = lax.broadcasted_iota(jnp.int32, (SUB, size), 1)
    sub = lax.broadcasted_iota(jnp.int32, (SUB, size), 0)
    pivots = [None] * groups
    for k in range(size):
        g0, k0 = divmod(k, SUB)
        at_k = lane == k
        cols = [jnp.broadcast_to(parts[g][:, k:k + 1], (SUB, size)) for g in range(g0, groups)]
        pivot = jnp.broadcast_to(cols[0][k0:k0 + 1, :], (SUB, size))
        row = jnp.broadcast_to(parts[g0][k0:k0 + 1, :], (SUB, size))
        inverse = 1.0 / pivot
        scaled = jnp.where(at_k, inverse, row * inverse)
        pivots[g0] = pivot if k0 == 0 else jnp.where(sub >= k0, pivot, pivots[g0])
        for g in range(g0, groups):
            updated = jnp.where(at_k, 0.0, parts[g]) - cols[g - g0] * scaled
            parts[g] = jnp.where(sub > k0, updated, parts[g]) if g == g0 else updated
    out = []
    for g in range(groups):
        below = jnp.where(lane < sub + g * SUB, parts[g], jnp.where(lane == sub + g * SUB, 1.0, 0.0))
        out.append(below * lax.rsqrt(pivots[g]))
    return jnp.concatenate(out, axis=0)


def kernel(n_row, n_col, rs_ref, fw_ref, di_ref, cov_ref, basis_ref, solved_ref,
           cov32, tile, rows, solved_all, bases,
           cov_send, cov_recv, f_send, f_fwd, f_recv, x_send, x_recv, b_send, b_recv):
    row = lax.axis_index("row")
    col = lax.axis_index("col")
    chips = n_col // CORES
    chip, core = col // CORES, col % CORES
    partner = chip * CORES + (1 - core)
    block = rs_ref.shape[0]
    width = fw_ref.shape[1]
    piece = cov32.shape[2]
    out_rows = bases.shape[1]

    barrier = pltpu.get_barrier_semaphore()
    for d in range(1, n_row):
        pl.semaphore_signal(barrier, inc=1, device_id=(lax.rem(row + d, n_row), col), device_id_type=MESH)
    for d in range(1, n_col):
        pl.semaphore_signal(barrier, inc=1, device_id=(row, lax.rem(col + d, n_col)), device_id_type=MESH)

    di = di_ref[...]
    rows[row, pl.ds(0, block), :] = dot_exact(rs_ref[...].T, di, NT)
    rows[row, pl.ds(block + col * width, width), :] = dot_exact(fw_ref[...].T, di, NT)
    for t in range(n_col):
        cov32[t] = cov_ref[:, t * piece:(t + 1) * piece].astype(F32)
    pl.semaphore_wait(barrier, n_row + n_col - 2)

    def f_copy(source, target, send):
        view = rows.at[row, pl.ds(block + source * width, width)]
        return pltpu.make_async_remote_copy(
            src_ref=view, dst_ref=view, send_sem=send, recv_sem=f_recv.at[source],
            device_id=(row, target), device_id_type=MESH)

    def far(d):
        return lax.rem(chip + d, chips) * CORES + core

    f_sends = [f_copy(col, far(d), f_send.at[d]) for d in range(1, chips)]
    f_sends.append(f_copy(col, partner, f_send.at[0]))
    for copy in f_sends:
        copy.start()

    def cov_copy(source, target, d):
        return pltpu.make_async_remote_copy(
            src_ref=cov32.at[target], dst_ref=tile.at[source],
            send_sem=cov_send.at[d], recv_sem=cov_recv.at[source],
            device_id=(row, target), device_id_type=MESH)

    order = sorted(range(1, n_col), key=lambda d: abs(2 * d - n_col))
    cov_sends = [cov_copy(col, lax.rem(col + d, n_col), d) for d in order]
    for copy in cov_sends:
        copy.start()
    tile[col] = cov32[col]

    forwards = []
    for d in range(1, chips):
        source = far(d)
        f_copy(source, partner, f_fwd.at[d]).wait_recv()
        copy = f_copy(source, partner, f_fwd.at[d])
        copy.start()
        forwards.append(copy)
    for d in range(chips):
        source = lax.rem(chip + d, chips) * CORES + (1 - core)
        f_copy(source, partner, f_fwd.at[0]).wait_recv()

    def x_copy(i, target, d):
        view = rows.at[i, pl.ds(0, (i + 1) * block)]
        return pltpu.make_async_remote_copy(
            src_ref=view, dst_ref=view, send_sem=x_send.at[d], recv_sem=x_recv.at[i],
            device_id=(target, col), device_id_type=MESH)

    for i in range(n_row):
        @pl.when(row == i)
        def _():
            for d in range(1, n_row):
                x_copy(i, (i + d) % n_row, d).start()

    solved = []
    for i in range(n_row):
        @pl.when(row != i)
        def _():
            x_copy(i, (i + 1) % n_row, 0).wait_recv()

        value = rows[i, pl.ds(0, block), :]
        if i:
            earlier = jnp.concatenate(solved, axis=1) if i > 1 else solved[0]
            value = value - dot_exact(earlier, rows[i, pl.ds(block, i * block), :], NN)
        solved.append(value)
        solved_all[pl.ds(i * block, block), :] = value.T
    solved_low = jnp.concatenate(solved, axis=1).astype(jnp.bfloat16)
    solved_ref[...] = solved_all[pl.ds(pl.multiple_of(col * width, width), width), :]

    for d in order:
        cov_copy(lax.rem(col + d, n_col), col, d).wait_recv()
    whole = tile[...].reshape(n_col * width, piece).astype(jnp.bfloat16)
    weighted = lax.dot_general(solved_low, whole, NN, preferred_element_type=F32)
    inverse = factor_inverse(dot_exact(weighted, weighted, NT))
    basis = dot_exact(weighted.T, inverse, NT)
    bases[...] = basis.reshape(bases.shape)

    def b_copy(source, target, d):
        return pltpu.make_async_remote_copy(
            src_ref=bases.at[target], dst_ref=basis_ref.at[source],
            send_sem=b_send.at[d], recv_sem=b_recv.at[source],
            device_id=(row, target), device_id_type=MESH)

    b_sends = [b_copy(col, lax.rem(col + d, n_col), d) for d in order]
    for copy in b_sends:
        copy.start()
    basis_ref[col] = bases[col]
    for copy in f_sends + forwards + cov_sends:
        copy.wait_send()
    for i in range(n_row):
        @pl.when(row == i)
        def _():
            for d in range(1, n_row):
                x_copy(i, (i + d) % n_row, d).wait_send()
    for d in order:
        b_copy(lax.rem(col + d, n_col), col, d).wait_recv()
    for copy in b_sends:
        copy.wait_send()


def solution(mesh):
    n_row, n_col = mesh.shape["row"], mesh.shape["col"]

    def local(right_side, factor_window, diag_inverse, phase_cov):
        block, rank = right_side.shape
        width = factor_window.shape[1]
        piece = phase_cov.shape[1] // n_col
        out_rows = piece // n_col
        vmem = pl.BlockSpec(memory_space=pltpu.VMEM)
        dma = pltpu.SemaphoreType.DMA
        return pl.pallas_call(
            functools.partial(kernel, n_row, n_col),
            out_shape=(
                jax.ShapeDtypeStruct((n_col, out_rows, rank), F32),
                jax.ShapeDtypeStruct((width, rank), F32),
            ),
            in_specs=[vmem] * 4,
            out_specs=(vmem, vmem),
            scratch_shapes=[
                pltpu.VMEM((n_col, width, piece), F32),
                pltpu.VMEM((n_col, width, piece), F32),
                pltpu.VMEM((n_row, (n_row + 1) * block, rank), F32),
                pltpu.VMEM((n_row * block, rank), F32),
                pltpu.VMEM((n_col, out_rows, rank), F32),
                dma((n_col,)), dma((n_col,)),
                dma((n_col,)), dma((n_col,)), dma((n_col,)),
                dma((n_row,)), dma((n_row,)),
                dma((n_col,)), dma((n_col,)),
            ],
            compiler_params=pltpu.CompilerParams(collective_id=0, has_side_effects=True),
        )(right_side, factor_window, diag_inverse, phase_cov)

    in_specs = (P("row", None), P("row", "col"), P("row", None), P("col", "row"))
    out_specs = (P("row", "col", None), P("col", None))
    return jax.shard_map(local, mesh=mesh, in_specs=in_specs, out_specs=out_specs, check_vma=False)
```

```python
import functools

import jax
import jax.numpy as jnp
from jax import lax
from jax.experimental import pallas as pl
from jax.experimental.pallas import tpu as pltpu
from jax.sharding import PartitionSpec as P

MESH = pl.DeviceIdType.MESH
CORES = 2
SUB = 8
F32 = jnp.float32
dot_exact = functools.partial(lax.dot_general, precision=lax.Precision.HIGHEST, preferred_element_type=F32)
NN = (((1,), (0,)), ((), ()))
NT = (((1,), (1,)), ((), ()))


def factor_inverse(gram):
    size = gram.shape[0]
    groups = size // SUB
    parts = [gram[g * SUB:(g + 1) * SUB, :] for g in range(groups)]
    lane = lax.broadcasted_iota(jnp.int32, (SUB, size), 1)
    sub = lax.broadcasted_iota(jnp.int32, (SUB, size), 0)
    spread = lambda x: jnp.broadcast_to(x, (SUB, size))
    out = []
    for g0 in range(groups):
        base = g0 * SUB
        inside = (lane >= base) & (lane < base + SUB)
        cols = [spread(parts[g0][:, base + j:base + j + 1]) for j in range(SUB)]
        entry = {(i, j): spread(cols[j][i:i + 1, :]) for i in range(SUB) for j in range(i + 1)}
        lines = [jnp.where(inside, jnp.where(lane == base + j, 1.0, 0.0), spread(parts[g0][j:j + 1, :])) for j in range(SUB)]
        ratio, inverses = {}, []
        for j in range(SUB):
            inverse = 1.0 / entry[j, j]
            inverses.append(inverse)
            for l in range(j + 1, SUB):
                ratio[l, j] = entry[l, j] * inverse
            for l in range(j + 1, SUB):
                for i in range(l, SUB):
                    entry[i, l] = entry[i, l] - entry[i, j] * ratio[l, j]
                lines[l] = lines[l] - ratio[l, j] * lines[j]
        scaled = [lines[j] * inverses[j] for j in range(SUB)]
        for g in range(g0 + 1, groups):
            left = [spread(parts[g][:, base + j:base + j + 1]) for j in range(SUB)]
            value = jnp.where(inside, 0.0, parts[g])
            for j in range(SUB):
                for l in range(j + 1, SUB):
                    left[l] = left[l] - left[j] * ratio[l, j]
                value = value - left[j] * scaled[j]
            parts[g] = value
        done, pivot = lines[0], entry[0, 0]
        for j in range(1, SUB):
            done = jnp.where(sub == j, lines[j], done)
            pivot = jnp.where(sub == j, entry[j, j], pivot)
        out.append(jnp.where(lane <= sub + base, done * lax.rsqrt(pivot), 0.0))
    return jnp.concatenate(out, axis=0)


def kernel(n_row, n_col, rs_ref, fw_ref, di_ref, cov_ref, basis_ref, solved_ref,
           cov32, tile, rows, solved_all, bases,
           cov_send, cov_recv, f_send, f_fwd, f_recv, x_send, x_recv, b_send, b_recv):
    row = lax.axis_index("row")
    col = lax.axis_index("col")
    chips = n_col // CORES
    chip, core = col // CORES, col % CORES
    partner = chip * CORES + (1 - core)
    block = rs_ref.shape[0]
    width = fw_ref.shape[0]
    piece = cov32.shape[2]

    barrier = pltpu.get_barrier_semaphore()
    for d in range(1, n_row):
        pl.semaphore_signal(barrier, inc=1, device_id=(lax.rem(row + d, n_row), col), device_id_type=MESH)
    for d in range(1, n_col):
        pl.semaphore_signal(barrier, inc=1, device_id=(row, lax.rem(col + d, n_col)), device_id_type=MESH)

    di = di_ref[...]
    rows[row, pl.ds(0, block), :] = dot_exact(rs_ref[...].T, di, NT)
    rows[row, pl.ds(block + col * width, width), :] = dot_exact(fw_ref[...], di, NT)
    for t in range(n_col):
        cov32[t] = cov_ref[:, t * piece:(t + 1) * piece].astype(F32)
    pl.semaphore_wait(barrier, n_row + n_col - 2)

    def f_copy(source, target, send):
        view = rows.at[row, pl.ds(block + source * width, width)]
        return pltpu.make_async_remote_copy(
            src_ref=view, dst_ref=view, send_sem=send, recv_sem=f_recv.at[source],
            device_id=(row, target), device_id_type=MESH)

    def far(d):
        return lax.rem(chip + d, chips) * CORES + core

    f_sends = [f_copy(col, far(d), f_send.at[d]) for d in range(1, chips)]
    f_sends.append(f_copy(col, partner, f_send.at[0]))
    for copy in f_sends:
        copy.start()

    def cov_copy(source, target, d):
        return pltpu.make_async_remote_copy(
            src_ref=cov32.at[target], dst_ref=tile.at[source],
            send_sem=cov_send.at[d], recv_sem=cov_recv.at[source],
            device_id=(row, target), device_id_type=MESH)

    order = sorted(range(1, n_col), key=lambda d: abs(2 * d - n_col))
    cov_sends = [cov_copy(col, lax.rem(col + d, n_col), d) for d in order]
    for copy in cov_sends:
        copy.start()
    tile[col] = cov32[col]

    forwards = []
    for d in range(1, chips):
        source = far(d)
        f_copy(source, partner, f_fwd.at[d]).wait_recv()
        copy = f_copy(source, partner, f_fwd.at[d])
        copy.start()
        forwards.append(copy)
    for d in range(chips):
        source = lax.rem(chip + d, chips) * CORES + (1 - core)
        f_copy(source, partner, f_fwd.at[0]).wait_recv()

    def x_copy(i, target, d):
        view = rows.at[i, pl.ds(0, (i + 1) * block)]
        return pltpu.make_async_remote_copy(
            src_ref=view, dst_ref=view, send_sem=x_send.at[d], recv_sem=x_recv.at[i],
            device_id=(target, col), device_id_type=MESH)

    for i in range(n_row):
        @pl.when(row == i)
        def _():
            for d in range(1, n_row):
                x_copy(i, (i + d) % n_row, d).start()

    solved = []
    for i in range(n_row):
        @pl.when(row != i)
        def _():
            x_copy(i, (i + 1) % n_row, 0).wait_recv()

        value = rows[i, pl.ds(0, block), :]
        if i:
            earlier = jnp.concatenate(solved, axis=1) if i > 1 else solved[0]
            value = value - dot_exact(earlier, rows[i, pl.ds(block, i * block), :], NN)
        solved.append(value)
        solved_all[pl.ds(i * block, block), :] = value.T
    solved_low = jnp.concatenate(solved, axis=1).astype(jnp.bfloat16)
    solved_ref[...] = solved_all[pl.ds(pl.multiple_of(col * width, width), width), :]

    for d in order:
        cov_copy(lax.rem(col + d, n_col), col, d).wait_recv()
    whole = tile[...].reshape(n_col * width, piece).astype(jnp.bfloat16)
    weighted = lax.dot_general(solved_low, whole, NN, preferred_element_type=F32)
    inverse = factor_inverse(dot_exact(weighted, weighted, NT))
    basis = dot_exact(weighted.T, inverse, NT)
    bases[...] = basis.reshape(bases.shape)

    def b_copy(source, target, d):
        return pltpu.make_async_remote_copy(
            src_ref=bases.at[target], dst_ref=basis_ref.at[source],
            send_sem=b_send.at[d], recv_sem=b_recv.at[source],
            device_id=(row, target), device_id_type=MESH)

    b_sends = [b_copy(col, lax.rem(col + d, n_col), d) for d in order]
    for copy in b_sends:
        copy.start()
    basis_ref[col] = bases[col]
    for copy in f_sends + forwards + cov_sends:
        copy.wait_send()
    for i in range(n_row):
        @pl.when(row == i)
        def _():
            for d in range(1, n_row):
                x_copy(i, (i + d) % n_row, d).wait_send()
    for d in order:
        b_copy(lax.rem(col + d, n_col), col, d).wait_recv()
    for copy in b_sends:
        copy.wait_send()


def solution(mesh):
    n_row, n_col = mesh.shape["row"], mesh.shape["col"]

    def local(right_side, factor_window, diag_inverse, phase_cov):
        block, rank = right_side.shape
        width = factor_window.shape[1]
        piece = phase_cov.shape[1] // n_col
        out_rows = piece // n_col
        vmem = pl.BlockSpec(memory_space=pltpu.VMEM)
        dma = pltpu.SemaphoreType.DMA
        return pl.pallas_call(
            functools.partial(kernel, n_row, n_col),
            out_shape=(
                pltpu.VMEM((n_col, out_rows, rank), F32),
                pltpu.VMEM((width, rank), F32),
            ),
            in_specs=[vmem] * 4,
            out_specs=(vmem, vmem),
            scratch_shapes=[
                pltpu.VMEM((n_col, width, piece), F32),
                pltpu.VMEM((n_col, width, piece), F32),
                pltpu.VMEM((n_row, (n_row + 1) * block, rank), F32),
                pltpu.VMEM((n_row * block, rank), F32),
                pltpu.VMEM((n_col, out_rows, rank), F32),
                dma((n_col,)), dma((n_col,)),
                dma((n_col,)), dma((n_col,)), dma((n_col,)),
                dma((n_row,)), dma((n_row,)),
                dma((n_col,)), dma((n_col,)),
            ],
            compiler_params=pltpu.CompilerParams(collective_id=0, has_side_effects=True),
        )(right_side, factor_window.T, diag_inverse, phase_cov)

    in_specs = (P("row", None), P("row", "col"), P("row", None), P("col", "row"))
    out_specs = (P("row", "col", None), P("col", None))
    return jax.shard_map(local, mesh=mesh, in_specs=in_specs, out_specs=out_specs, check_vma=False)
```

```python
import functools

import jax
import jax.numpy as jnp
from jax import lax
from jax.experimental import pallas as pl
from jax.experimental.pallas import tpu as pltpu
from jax.sharding import PartitionSpec as P

MESH = pl.DeviceIdType.MESH
CORES = 2
SUB = 8
F32 = jnp.float32
dot_exact = functools.partial(lax.dot_general, precision=lax.Precision.HIGHEST, preferred_element_type=F32)
NN = (((1,), (0,)), ((), ()))
NT = (((1,), (1,)), ((), ()))


def halves(x):
    high = x.astype(jnp.bfloat16)
    return high, (x - high.astype(F32)).astype(jnp.bfloat16)


def dot_low(a, b):
    return lax.dot_general(a, b, NT, preferred_element_type=F32)


def factor_inverse(gram):
    size = gram.shape[0]
    groups = size // SUB
    parts = [gram[g * SUB:(g + 1) * SUB, :] for g in range(groups)]
    lane = lax.broadcasted_iota(jnp.int32, (SUB, size), 1)
    sub = lax.broadcasted_iota(jnp.int32, (SUB, size), 0)
    spread = lambda x: jnp.broadcast_to(x, (SUB, size))
    out = []
    for g0 in range(groups):
        base = g0 * SUB
        inside = (lane >= base) & (lane < base + SUB)
        cols = [spread(parts[g0][:, base + j:base + j + 1]) for j in range(SUB)]
        entry = {(i, j): spread(cols[j][i:i + 1, :]) for i in range(SUB) for j in range(i + 1)}
        lines = [jnp.where(inside, jnp.where(lane == base + j, 1.0, 0.0), spread(parts[g0][j:j + 1, :])) for j in range(SUB)]
        ratio, inverses = {}, []
        for j in range(SUB):
            inverse = 1.0 / entry[j, j]
            inverses.append(inverse)
            for l in range(j + 1, SUB):
                ratio[l, j] = entry[l, j] * inverse
            for l in range(j + 1, SUB):
                for i in range(l, SUB):
                    entry[i, l] = entry[i, l] - entry[i, j] * ratio[l, j]
                lines[l] = lines[l] - ratio[l, j] * lines[j]
        scaled = [lines[j] * inverses[j] for j in range(SUB)]
        for g in range(g0 + 1, groups):
            left = [spread(parts[g][:, base + j:base + j + 1]) for j in range(SUB)]
            value = jnp.where(inside, 0.0, parts[g])
            for j in range(SUB):
                for l in range(j + 1, SUB):
                    left[l] = left[l] - left[j] * ratio[l, j]
                value = value - left[j] * scaled[j]
            parts[g] = value
        done, pivot = lines[0], entry[0, 0]
        for j in range(1, SUB):
            done = jnp.where(sub == j, lines[j], done)
            pivot = jnp.where(sub == j, entry[j, j], pivot)
        out.append(jnp.where(lane <= sub + base, done * lax.rsqrt(pivot), 0.0))
    return jnp.concatenate(out, axis=0)


def kernel(n_row, n_col, rs_ref, fw_ref, di_ref, cov_ref, basis_ref, solved_ref,
           cov_low, cov32, tile, rows, solved_all, bases, wide,
           cov_load, cov_send, cov_recv, f_send, f_fwd, f_pass, f_recv, x_send, x_recv, x_fwd, x_other, b_send, b_recv):
    row = lax.axis_index("row")
    col = lax.axis_index("col")
    chips = n_col // CORES
    chip, core = col // CORES, col % CORES
    partner = chip * CORES + (1 - core)
    block = rs_ref.shape[0]
    width = fw_ref.shape[0]
    piece = cov32.shape[2]
    out_rows = bases.shape[1]

    load = pltpu.make_async_copy(cov_ref, cov_low, cov_load)
    load.start()
    barrier = pltpu.get_barrier_semaphore()
    for d in range(1, n_row):
        pl.semaphore_signal(barrier, inc=1, device_id=(lax.rem(row + d, n_row), col), device_id_type=MESH)
    for d in range(1, n_col):
        pl.semaphore_signal(barrier, inc=1, device_id=(row, lax.rem(col + d, n_col)), device_id_type=MESH)

    di = di_ref[...]
    rows[row, pl.ds(0, block), :] = dot_exact(rs_ref[...].T, di, NT)
    rows[row, pl.ds(block + col * width, width), :] = dot_exact(fw_ref[...], di, NT)
    load.wait()
    for t in range(n_col):
        cov32[t] = cov_low[:, t * piece:(t + 1) * piece].astype(F32)
    pl.semaphore_wait(barrier, n_row + n_col - 2)

    def f_copy(source, target, send):
        view = rows.at[row, pl.ds(block + source * width, width)]
        return pltpu.make_async_remote_copy(
            src_ref=view, dst_ref=view, send_sem=send, recv_sem=f_recv.at[source],
            device_id=(row, target), device_id_type=MESH)

    quarter = chips // 4
    inner = range(quarter, chips - quarter)
    is_inner = (chip >= quarter) & (chip < chips - quarter)
    outer = chip + quarter * (2 * (chip // (chips // 2)) - 1)

    def to_outer(q):
        return f_copy(q * CORES + core, outer * CORES + core, f_pass.at[q])

    for q in inner:
        @pl.when(chip != q)
        def _():
            f_copy(col, q * CORES + core, f_send.at[q]).start()
    f_copy(col, partner, f_send.at[chips]).start()
    if quarter:
        @pl.when(is_inner)
        def _():
            f_copy(col, outer * CORES + core, f_send.at[chips + 1]).start()

    def cov_copy(source, target, d):
        return pltpu.make_async_remote_copy(
            src_ref=cov32.at[target], dst_ref=tile.at[source],
            send_sem=cov_send.at[d], recv_sem=cov_recv.at[source],
            device_id=(row, target), device_id_type=MESH)

    order = sorted(range(1, n_col), key=lambda d: abs(2 * d - n_col))
    cov_sends = [cov_copy(col, lax.rem(col + d, n_col), d) for d in order]
    late = [is_inner & (lax.rem(col + d, n_col) // CORES == outer) for d in order]
    for copy, wait in zip(cov_sends, late):
        @pl.when(jnp.logical_not(wait))
        def _():
            copy.start()
    tile[col] = cov32[col]

    for q in range(chips):
        @pl.when(chip != q)
        def _():
            f_copy(q * CORES + core, partner, f_fwd.at[q]).wait_recv()
            if quarter:
                @pl.when(is_inner & (outer != q))
                def _():
                    to_outer(q).start()
            f_copy(q * CORES + core, partner, f_fwd.at[q]).start()
    for copy, wait in zip(cov_sends, late):
        @pl.when(wait)
        def _():
            copy.start()
    for q in range(chips):
        f_copy(q * CORES + (1 - core), partner, f_fwd.at[q]).wait_recv()

    def x_half(i, part):
        size = (i + 1) * block // CORES
        return rows.at[i, pl.ds(pl.multiple_of(part * size, SUB), size)]

    def x_copy(i, target, d):
        return pltpu.make_async_remote_copy(
            src_ref=x_half(i, core), dst_ref=x_half(i, core),
            send_sem=x_send.at[d], recv_sem=x_recv.at[i],
            device_id=(target, col), device_id_type=MESH)

    def x_pass(i, part):
        return pltpu.make_async_remote_copy(
            src_ref=x_half(i, part), dst_ref=x_half(i, part),
            send_sem=x_fwd.at[i], recv_sem=x_other.at[i],
            device_id=(row, partner), device_id_type=MESH)

    for i in range(n_row):
        @pl.when(row == i)
        def _():
            for d in range(1, n_row):
                x_copy(i, (i + d) % n_row, d).start()

    for i in range(n_row):
        @pl.when(row != i)
        def _():
            x_copy(i, (i + 1) % n_row, 0).wait_recv()
            x_pass(i, core).start()

    solved = []
    for i in range(n_row):
        @pl.when(row != i)
        def _():
            x_pass(i, 1 - core).wait_recv()

        value = rows[i, pl.ds(0, block), :]
        if i:
            earlier = jnp.concatenate(solved, axis=1) if i > 1 else solved[0]
            value = value - dot_exact(earlier, rows[i, pl.ds(block, i * block), :], NN)
        solved.append(value)
        solved_all[pl.ds(i * block, block), :] = value.T
    solved_low = jnp.concatenate(solved, axis=1).astype(jnp.bfloat16)
    solved_ref[...] = solved_all[pl.ds(pl.multiple_of(col * width, width), width), :]

    for d in order:
        cov_copy(lax.rem(col + d, n_col), col, d).wait_recv()
    whole = tile[...].reshape(n_col * width, piece).astype(jnp.bfloat16)
    weighted = lax.dot_general(solved_low, whole, NN, preferred_element_type=F32)
    wide[...] = weighted.T
    inverse = factor_inverse(dot_exact(weighted, weighted, NT))
    inverse_high, inverse_low = halves(inverse)

    def b_copy(source, target, d):
        return pltpu.make_async_remote_copy(
            src_ref=bases.at[target], dst_ref=basis_ref.at[source],
            send_sem=b_send.at[d], recv_sem=b_recv.at[source],
            device_id=(row, target), device_id_type=MESH)

    def basis_rows(targets):
        taken = jnp.concatenate([wide[pl.ds(pl.multiple_of(t * out_rows, out_rows), out_rows), :] for t in targets], axis=0)
        high, low = halves(taken)
        found = dot_low(high, inverse_high) + (dot_low(high, inverse_low) + dot_low(low, inverse_high))
        return [found[j * out_rows:(j + 1) * out_rows, :] for j in range(len(targets))]

    b_sends = []
    half = n_col // 2
    for chosen in (order[:half], order[half:]):
        targets = [lax.rem(col + d, n_col) for d in chosen]
        found = basis_rows(targets if len(chosen) == half else targets + [col])
        for d, target, value in zip(chosen, targets, found):
            bases[target] = value
        for d, target in zip(chosen, targets):
            copy = b_copy(col, target, d)
            copy.start()
            b_sends.append(copy)
        if len(found) > len(chosen):
            basis_ref[col] = found[-1]
    for copy in cov_sends:
        copy.wait_send()
    for q in inner:
        @pl.when(chip != q)
        def _():
            f_copy(col, q * CORES + core, f_send.at[q]).wait_send()
    f_copy(col, partner, f_send.at[chips]).wait_send()
    if quarter:
        @pl.when(is_inner)
        def _():
            f_copy(col, outer * CORES + core, f_send.at[chips + 1]).wait_send()
    for q in range(chips):
        @pl.when(chip != q)
        def _():
            f_copy(q * CORES + core, partner, f_fwd.at[q]).wait_send()
            if quarter:
                @pl.when(is_inner & (outer != q))
                def _():
                    to_outer(q).wait_send()
    for i in range(n_row):
        @pl.when(row == i)
        def _():
            for d in range(1, n_row):
                x_copy(i, (i + d) % n_row, d).wait_send()

        @pl.when(row != i)
        def _():
            x_pass(i, core).wait_send()
    for d in order:
        b_copy(lax.rem(col + d, n_col), col, d).wait_recv()
    for copy in b_sends:
        copy.wait_send()


def solution(mesh):
    n_row, n_col = mesh.shape["row"], mesh.shape["col"]

    def local(right_side, factor_window, diag_inverse, phase_cov):
        block, rank = right_side.shape
        width = factor_window.shape[1]
        piece = phase_cov.shape[1] // n_col
        out_rows = piece // n_col
        vmem = pl.BlockSpec(memory_space=pltpu.VMEM)
        dma = pltpu.SemaphoreType.DMA
        return pl.pallas_call(
            functools.partial(kernel, n_row, n_col),
            out_shape=(
                pltpu.VMEM((n_col, out_rows, rank), F32),
                pltpu.VMEM((width, rank), F32),
            ),
            in_specs=[vmem] * 3 + [pl.BlockSpec(memory_space=pl.ANY)],
            out_specs=(vmem, vmem),
            scratch_shapes=[
                pltpu.VMEM(phase_cov.shape, phase_cov.dtype),
                pltpu.VMEM((n_col, width, piece), F32),
                pltpu.VMEM((n_col, width, piece), F32),
                pltpu.VMEM((n_row, (n_row + 1) * block, rank), F32),
                pltpu.VMEM((n_row * block, rank), F32),
                pltpu.VMEM((n_col, out_rows, rank), F32),
                pltpu.VMEM((piece, rank), F32),
                dma, dma((n_col,)), dma((n_col,)),
                dma((n_col + 2,)), dma((n_col,)), dma((n_col,)), dma((n_col,)),
                dma((n_row,)), dma((n_row,)), dma((n_row,)), dma((n_row,)),
                dma((n_col,)), dma((n_col,)),
            ],
            compiler_params=pltpu.CompilerParams(collective_id=0, has_side_effects=True),
        )(right_side, factor_window.T, diag_inverse, phase_cov)

    in_specs = (P("row", None), P("row", "col"), P("row", None), P("col", "row"))
    out_specs = (P("row", "col", None), P("col", None))
    return jax.shard_map(local, mesh=mesh, in_specs=in_specs, out_specs=out_specs, check_vma=False)
```
